256 devices in a mesh: shot: 64 (over y, z_hi, x), rcv: 4 (over z_lo, core).
Axes of the slice: x: 4, y: 4, z: 8 (z_hi: 4, z_lo: 2; z = z_hi * 2 + z_lo), core: 2. Of those that a mesh axis runs over, the one named last changes fastest.
Arguments:
- data: bfloat16 [384, 1024, 256], P('shot', 'rcv'), may hold values from -6 to 6
- surface_traces: bfloat16 [1024, 1024, 256], P('shot', 'rcv'), may hold values from -6 to 6
- primaries: bfloat16 [384, 64, 64], P('shot', 'rcv'), may hold values from -0.09375 to 0.09375
- panel_owner: int32 [4], replicated, may hold values from 0 to 63, as said below
Outputs:
- residual: bfloat16 [384, 1024, 256], P('shot', 'rcv')
The draws below stay inside these ranges and needn't reach their ends.
Inputs may be any that keep to these rules, and one draw needn't show every extreme that they name: panel_owner holds 4 distinct indices of the shot axis, in an order drawn from the seed.
All inputs are finite; a program needn't handle non-finite values.
Results may differ from the reference program's by a relative error of at most 0.001.
Values may be sent and summed in bfloat16 or wider, within the bound.
A program may use at most 128 MiB of HBM per device.

```python
import jax
import jax.numpy as jnp
from jax import lax

R = 1024
T_SIZE = 256
TAPS = 64
KP = 16
PANELS = 4
K = 64
SHOTS = 384
SLOTS = 1024
N_SHOT = 64


def draw_panel_owner(key, part):
    first_key = jax.random.fold_in(key, 11)
    second_key = jax.random.fold_in(key, 23)
    middle = jax.random.permutation(first_key, N_SHOT - 2)[:PANELS - 2] + 1
    chosen = jnp.concatenate([jnp.array([0, N_SHOT - 1], jnp.int32), middle.astype(jnp.int32)])
    return jax.random.permutation(second_key, chosen).astype(jnp.int32)


def block_scale(key, dims, cuts, low, high):
    gain = 1.0
    for dim, shards_of in cuts:
        steps = jax.random.uniform(jax.random.fold_in(jax.random.fold_in(key, 6), dim), (shards_of,), jnp.float32, low / len(cuts), high / len(cuts))
        gain = gain * jnp.repeat(jnp.exp(steps), dims[dim] // shards_of).reshape((-1,) + (1,) * (len(dims) - 1 - dim))
    return gain


def centred(stream_key, extent, spread, limit, pieces=(), held_as=jnp.bfloat16):
    values = jax.random.normal(stream_key, extent, jnp.float32) * spread
    if len(pieces) > 0:
        values = block_scale(stream_key, extent, pieces, -0.22, 0.18) * values
    return jnp.clip(values, min=-limit, max=limit).astype(held_as)


def setup_inputs(seed: int = 0) -> dict:
    splits = jax.random.split(jax.random.key(seed), 5)
    data = centred(splits[0], (SHOTS, R, T_SIZE), 1.0, 6.0, ((0, 64), (1, 4)))
    surface_traces = centred(splits[1], (SLOTS, R, T_SIZE), 1.0, 6.0, ((0, 64), (1, 4)))
    primaries = centred(splits[2], (SHOTS, K, TAPS), (K * TAPS) ** -0.5, 0.09375, ((0, 64), (1, 4)))
    panel_owner = draw_panel_owner(jax.random.fold_in(splits[4], 71), 0)
    return dict(data=data, surface_traces=surface_traces, primaries=primaries, panel_owner=panel_owner)


def reference(data, surface_traces, primaries, panel_owner):
    owner_slots = surface_traces.reshape(N_SHOT, KP, R, T_SIZE)
    window = jnp.take(owner_slots, panel_owner.astype(jnp.int32), axis=0).reshape(K, R, T_SIZE)
    length = 2 * T_SIZE
    window_freq = jnp.fft.rfft(window.astype(jnp.float32), n=length, axis=-1)
    prim_freq = jnp.fft.rfft(primaries.astype(jnp.float32), n=length, axis=-1)

    def one_shot(spectra):
        mult_freq = jnp.einsum('kf,krf->rf', spectra, window_freq)
        return jnp.fft.irfft(mult_freq, n=length, axis=-1)[:, :T_SIZE]

    multiples = lax.map(one_shot, prim_freq)
    return (data.astype(jnp.float32) - multiples).astype(jnp.bfloat16)
```

```python
import functools

import jax
import jax.numpy as jnp
from jax import lax
from jax.experimental import pallas as pl
from jax.experimental.pallas import tpu as pltpu
from jax.sharding import PartitionSpec as P

NY, NZ, NX = 4, 4, 4
NR = 4
PLANE = NY * NX
TAPS = 64
LANES = 128
CHUNKS = 4


def shot_index(y, z, x):
    return (y * NZ + z) * NX + x


def kernel(owner, traces, prim_in, data, out, ra, sb, rb, win, prim, prim32, band, acc,
           own_sem, pa_send, pa_recv, pb_send, pb_recv, zg_send, zg_recv,
           pr_own, pr_send, pr_recv, xy_send, s1, f1, s2, f2):
    rows = data.shape[1]
    shots = data.shape[0]
    size = rows // CHUNKS
    shot = lax.axis_index("shot")
    rcv = lax.axis_index("rcv")
    my_x = lax.rem(shot, NX)
    my_z = lax.rem(shot // NX, NZ)
    my_y = shot // (NX * NZ)
    my_q = my_y * NX + my_x

    def at(dy, dz, dx):
        y = lax.rem(my_y + dy, NY)
        z = lax.rem(my_z + dz, NZ)
        x = lax.rem(my_x + dx, NX)
        return shot_index(y, z, x), y * NX + x, z

    plane = [(dy, dx) for dy in range(NY) for dx in range(NX) if dy or dx]
    order = sorted(plane, key=lambda d: -(min(d[0], NY - d[0]) + min(d[1], NX - d[1])))

    barrier = pltpu.get_barrier_semaphore()
    for dy, dx in plane:
        pl.semaphore_signal(barrier, inc=1, device_id={"shot": at(dy, 0, dx)[0]})
    for dz in range(1, NZ):
        pl.semaphore_signal(barrier, inc=1, device_id={"shot": at(0, dz, 0)[0]})
    for dr in range(1, NR):
        pl.semaphore_signal(barrier, inc=1, device_id={"rcv": lax.rem(rcv + dr, NR)})
    pl.semaphore_wait(barrier, len(plane) + NZ - 1 + NR - 1)

    def part(c):
        return pl.ds(c * size, size)

    pltpu.make_async_copy(prim_in, prim.at[rcv], pr_own).start()
    for dr in range(1, NR):
        pltpu.make_async_remote_copy(
            src_ref=prim_in, dst_ref=prim.at[rcv], send_sem=pr_send.at[dr], recv_sem=pr_recv.at[dr],
            device_id={"rcv": lax.rem(rcv + dr, NR)}).start()

    for c in range(CHUNKS):
        pltpu.make_async_copy(traces.at[my_q, part(c)], ra[c].at[my_q], own_sem.at[c]).start()
        for dy, dx in order:
            device, q, _ = at(dy, 0, dx)
            pltpu.make_async_remote_copy(
                src_ref=traces.at[q, part(c)], dst_ref=ra[c].at[my_q],
                send_sem=pa_send.at[c], recv_sem=pa_recv.at[c], device_id={"shot": device}).start()

    pltpu.make_async_copy(prim_in, prim.at[rcv], pr_own).wait()
    for dr in range(1, NR):
        pltpu.make_async_copy(prim_in, prim.at[0], pr_recv.at[dr]).wait()
    prim32[...] = jnp.zeros_like(prim32)
    prim32[:, :, :, 0:TAPS] = prim[...].astype(jnp.float32)

    def make_bands(q, carry):
        for h in range(4):
            for s in range(shots):
                row = prim32[h, s, pl.ds(q, 1), :]
                tile = pltpu.roll(jnp.broadcast_to(row, (TAPS, LANES)), 0, 1, stride=1, stride_axis=0)
                start = pl.multiple_of(q * (4 * TAPS) + h * TAPS, TAPS)
                band[pl.ds(start, TAPS), s * LANES:(s + 1) * LANES] = tile.astype(jnp.bfloat16)
        return carry

    lax.fori_loop(0, PLANE, make_bands, 0)

    def gathered(buffer, count, sem, c):
        piece = buffer.at[pl.ds(0, count), part(c)]
        pltpu.make_async_copy(piece, piece, sem).wait()

    def split(index):
        return index // (NX * NZ) * NX + lax.rem(index, NX), lax.rem(index // NX, NZ)

    def stage_plane(c):
        pltpu.make_async_copy(traces.at[0, part(c)], ra[c].at[0], own_sem.at[c]).wait()
        gathered(win, PLANE - 1, pa_recv.at[c], c)
        for h in range(NZ):
            sb[h, part(c)] = ra[c][split(owner[h])[0]]
        for dz in range(1, NZ):
            device, _, z = at(0, dz, 0)
            pltpu.make_async_remote_copy(
                src_ref=sb.at[z, part(c)], dst_ref=rb[c].at[my_z],
                send_sem=pb_send.at[c], recv_sem=pb_recv.at[c], device_id={"shot": device}).start()
        rb[c][my_z] = sb[my_z, part(c)]

    def stage_column(c):
        gathered(win, NZ - 1, pb_recv.at[c], c)
        mine = my_q * NZ + my_z
        win[mine, part(c)] = rb[c][split(owner[my_z])[1]]
        for dz in range(1, NZ):
            device, _, _ = at(0, dz, 0)
            piece = win.at[mine, part(c)]
            pltpu.make_async_remote_copy(
                src_ref=piece, dst_ref=piece,
                send_sem=zg_send.at[c], recv_sem=zg_recv.at[c], device_id={"shot": device}).start()

    def step(kind, first, second):
        return (second, first) if kind == 0 else (first, second)

    def place(kind, first, second):
        dy, dx = step(kind, first, second)
        device, q, _ = at(dy, 0, dx)
        return device, q

    def send(q, low, count, c, sem, device):
        piece = win.at[pl.ds(q * NZ + low, count), part(c)]
        pltpu.make_async_remote_copy(
            src_ref=piece, dst_ref=piece, send_sem=xy_send.at[c], recv_sem=sem,
            device_id={"shot": device}).start()

    def arrive(q, low, count, c, sem):
        piece = win.at[pl.ds(q * NZ + low, count), part(c)]
        pltpu.make_async_copy(piece, piece, sem).wait()

    def spread(kind, hop, c):
        _, q = place(kind, hop, 0)
        for side, away in ((0, 1), (1, 3)):
            send(q, 2 * kind, 2, c, s2.at[c, kind, side, hop], place(kind, 0, away)[0])

    def stage_own(c):
        gathered(win, NZ - 1, zg_recv.at[c], c)
        for kind in range(2):
            _, q = place(kind, 0, 0)
            for side, away in ((0, 1), (1, 3)):
                send(q, 2 * kind, 2, c, s1.at[c, kind, side], place(kind, away, 0)[0])
        for kind in range(2):
            spread(kind, 0, c)

    def stage_near(c):
        for kind in range(2):
            for side, away in ((0, 1), (1, 3)):
                back = 4 - away
                _, q = place(kind, back, 0)
                arrive(q, 2 * kind, 2, c, s1.at[c, kind, side])
                send(q, 2 * kind + side, 1, c, f1.at[c, kind, side], place(kind, away, 0)[0])
                spread(kind, back, c)

    def stage_far(c):
        for kind in range(2):
            _, q = place(kind, 2, 0)
            for side in range(2):
                arrive(q, 2 * kind + side, 1, c, f1.at[c, kind, side])
            spread(kind, 2, c)

    hops = (0, 3, 1, 2)

    def stage_second(c):
        for hop in hops:
            for kind in range(2):
                for side, away in ((0, 1), (1, 3)):
                    back = 4 - away
                    _, q = place(kind, hop, back)
                    arrive(q, 2 * kind, 2, c, s2.at[c, kind, side, hop])
                    send(q, 2 * kind + side, 1, c, f2.at[c, kind, side, hop], place(kind, 0, away)[0])

    def stage_last(c):
        for hop in hops:
            for kind in range(2):
                _, q = place(kind, hop, 2)
                for side in range(2):
                    arrive(q, 2 * kind + side, 1, c, f2.at[c, kind, side, hop])

    def compute(c):
        acc[...] = jnp.zeros_like(acc)

        def body(q, carry):
            tiles = [win[q * NZ + h, part(c)] for h in range(4)]
            lhs = jnp.concatenate(
                [jnp.concatenate([x[:, b * TAPS:(b + 1) * TAPS] for x in tiles], axis=1) for b in range(4)], axis=0)
            start = pl.multiple_of(q * (4 * TAPS), 4 * TAPS)
            acc[...] += jnp.dot(lhs, band[pl.ds(start, 4 * TAPS), :], preferred_element_type=jnp.float32)
            return carry

        lax.fori_loop(0, PLANE, body, 0)
        lane = lax.broadcasted_iota(jnp.int32, (size, LANES), 1)
        for s in range(shots):
            cols = slice(s * LANES, (s + 1) * LANES)
            a = [acc[b * size:(b + 1) * size, cols] for b in range(4)]
            odd, last = pltpu.roll(a[1], TAPS, 1), pltpu.roll(a[3], TAPS, 1)
            low = a[0] + jnp.where(lane >= TAPS, odd, 0.0)
            high = a[2] + jnp.where(lane < TAPS, odd, last)
            for half, value in ((0, low), (1, high)):
                span = slice(half * LANES, (half + 1) * LANES)
                out[s, part(c), span] = (data[s, part(c), span].astype(jnp.float32) - value).astype(jnp.bfloat16)

    last = CHUNKS - 1
    stage_plane(0)
    stage_column(0)
    stage_plane(1)
    stage_own(0)
    stage_column(1)
    stage_near(0)
    stage_plane(2)
    stage_own(1)
    stage_far(0)
    stage_column(2)
    stage_near(1)
    stage_second(0)
    stage_plane(3)
    stage_own(2)
    stage_far(1)
    stage_column(3)
    stage_near(2)
    stage_last(0)
    stage_second(1)
    stage_own(3)
    stage_far(2)
    compute(0)
    stage_near(3)
    stage_last(1)
    stage_second(2)
    stage_far(3)
    compute(1)
    stage_last(2)
    stage_second(3)
    compute(2)
    stage_last(3)
    compute(3)

    for dr in range(1, NR):
        pltpu.make_async_copy(prim_in, prim.at[0], pr_send.at[dr]).wait()
    for c in range(CHUNKS):
        gathered(win, PLANE - 1, pa_send.at[c], c)
        gathered(win, NZ - 1, pb_send.at[c], c)
        gathered(win, NZ - 1, zg_send.at[c], c)
        gathered(win, 60, xy_send.at[c], c)


def shards(data, surface_traces, primaries, panel_owner):
    shots, rows, length = data.shape
    points = surface_traces.shape[0]
    size = rows // CHUNKS
    dma = pltpu.SemaphoreType.DMA
    vmem = pl.BlockSpec(memory_space=pltpu.VMEM)
    return pl.pallas_call(
        kernel,
        out_shape=jax.ShapeDtypeStruct(data.shape, jnp.bfloat16),
        in_specs=[pl.BlockSpec(memory_space=pltpu.SMEM), pl.BlockSpec(memory_space=pl.ANY), vmem, vmem],
        out_specs=vmem,
        scratch_shapes=[
            [pltpu.VMEM((PLANE, size, length), jnp.bfloat16)] * CHUNKS,
            pltpu.VMEM((NZ, rows, length), jnp.bfloat16),
            [pltpu.VMEM((NZ, size, length), jnp.bfloat16)] * CHUNKS,
            pltpu.VMEM((PLANE * NZ, rows, length), jnp.bfloat16),
            pltpu.VMEM((NR,) + primaries.shape, jnp.bfloat16),
            pltpu.VMEM((NR, shots, points, LANES), jnp.float32),
            pltpu.VMEM((PLANE * 4 * TAPS, shots * LANES), jnp.bfloat16),
            pltpu.VMEM((4 * size, shots * LANES), jnp.float32),
            dma((CHUNKS,)), dma((CHUNKS,)), dma((CHUNKS,)), dma((CHUNKS,)), dma((CHUNKS,)), dma((CHUNKS,)), dma((CHUNKS,)),
            dma, dma((NR,)), dma((NR,)),
            dma((CHUNKS,)), dma((CHUNKS, 2, 2)), dma((CHUNKS, 2, 2)), dma((CHUNKS, 2, 2, 4)), dma((CHUNKS, 2, 2, 4)),
        ],
        compiler_params=pltpu.CompilerParams(
            collective_id=0, has_side_effects=True, vmem_limit_bytes=60 * 1024 * 1024),
    )(panel_owner, surface_traces, primaries, data)


def solution(mesh):
    placed = (P("shot", "rcv", None), P("shot", "rcv", None), P("shot", "rcv", None), P())
    return jax.shard_map(
        shards, mesh=mesh, in_specs=placed, out_specs=P("shot", "rcv", None), check_vma=False
    )
```

```python
import jax
import jax.numpy as jnp
from jax import lax
from jax.experimental import pallas as pl
from jax.experimental.pallas import tpu as pltpu
from jax.sharding import PartitionSpec as P

NY, NZ, NX = 4, 4, 4
NR = 4
PLANE = NY * NX
TAPS = 64
LANES = 128
CHUNKS = 4


def kernel(owner, traces, prim_in, data, out, ra, sb, rb, win, prim, prim32, band, lhs, acc, held, res,
           own_sem, pa_send, pa_recv, pb_send, pb_recv, zg_send, zg_recv,
           px_own, px_send, px_recv, pr_send, pr_recv, y_send, y1, y2, d_own, d_send, d_recv, o_own, o_send, o_recv):
    shots, rows, length = data.shape
    size = rows // NX
    wide = shots * LANES
    deep = NY * 4 * TAPS
    shot = lax.axis_index("shot")
    rcv = lax.axis_index("rcv")
    my_x = lax.rem(shot, NX)
    my_z = lax.rem(shot // NX, NZ)
    my_y = shot // (NX * NZ)
    my_q = my_y * NX + my_x

    def at(dy, dz, dx):
        y = lax.rem(my_y + dy, NY)
        z = lax.rem(my_z + dz, NZ)
        x = lax.rem(my_x + dx, NX)
        return (y * NZ + z) * NX + x, y, z, x

    def part(x):
        return pl.ds(pl.multiple_of(x * size, size), size)

    plane = [(dy, dx) for dy in range(NY) for dx in range(NX) if dy or dx]
    order = sorted(plane, key=lambda d: -(min(d[0], NY - d[0]) + min(d[1], NX - d[1])))

    barrier = pltpu.get_barrier_semaphore()
    for dy, dx in plane:
        pl.semaphore_signal(barrier, inc=1, device_id={"shot": at(dy, 0, dx)[0]})
    for dz in range(1, NZ):
        pl.semaphore_signal(barrier, inc=1, device_id={"shot": at(0, dz, 0)[0]})
    for dr in range(1, NR):
        pl.semaphore_signal(barrier, inc=1, device_id={"rcv": lax.rem(rcv + dr, NR)})
    pltpu.make_async_copy(prim_in, prim.at[rcv, my_x], px_own).start()
    for c in range(CHUNKS):
        pltpu.make_async_copy(traces.at[my_y * 4 + c, part(my_x)], ra[c].at[my_q], own_sem.at[c]).start()
    pltpu.make_async_copy(data.at[:, part(my_x)], held.at[my_x], d_own).start()
    pl.semaphore_wait(barrier, len(plane) + NZ - 1 + NR - 1)

    for dx in range(1, NX):
        pltpu.make_async_remote_copy(
            src_ref=prim_in, dst_ref=prim.at[rcv, my_x], send_sem=px_send.at[dx], recv_sem=px_recv.at[dx],
            device_id={"shot": at(0, 0, dx)[0]}).start()

    for c in range(CHUNKS):
        for dy, dx in order:
            device, y, _, x = at(dy, 0, dx)
            pltpu.make_async_remote_copy(
                src_ref=traces.at[y * 4 + c, part(x)], dst_ref=ra[c].at[my_q],
                send_sem=pa_send.at[c], recv_sem=pa_recv.at[c], device_id={"shot": device}).start()

    for dx in (2, 1, 3):
        device, _, _, x = at(0, 0, dx)
        pltpu.make_async_remote_copy(
            src_ref=data.at[:, part(x)], dst_ref=held.at[my_x], send_sem=d_send.at[dx], recv_sem=d_recv.at[dx],
            device_id={"shot": device}).start()

    def responses_x():
        pltpu.make_async_copy(prim_in, prim.at[rcv, my_x], px_own).wait()
        for dx in range(1, NX):
            pltpu.make_async_copy(prim_in, prim.at[rcv, my_x], px_recv.at[dx]).wait()
        for dr in range(1, NR):
            pltpu.make_async_remote_copy(
                src_ref=prim.at[rcv], dst_ref=prim.at[rcv], send_sem=pr_send.at[dr], recv_sem=pr_recv.at[dr],
                device_id={"rcv": lax.rem(rcv + dr, NR)}).start()

    def responses_rcv():
        for dr in range(1, NR):
            pltpu.make_async_copy(prim.at[0], prim.at[0], pr_recv.at[dr]).wait()
        prim32[...] = jnp.zeros_like(prim32)
        prim32[:, :, :, :, 0:TAPS] = prim[...].astype(jnp.float32)

    def make_bands(c):
        def body(step, carry):
            x, y = step // NY, lax.rem(step, NY)
            for h in range(4):
                for s in range(shots):
                    row = prim32[h, x, s, pl.ds(y * 4 + c, 1), :]
                    tile = pltpu.roll(jnp.broadcast_to(row, (TAPS, LANES)), 0, 1, stride=1, stride_axis=0)
                    start = pl.multiple_of(c * deep + y * (4 * TAPS) + h * TAPS, TAPS)
                    band[x, pl.ds(start, TAPS), s * LANES:(s + 1) * LANES] = tile.astype(jnp.bfloat16)
            return carry

        lax.fori_loop(0, NX * NY, body, 0)

    def gathered(count, sem):
        piece = win.at[pl.ds(0, count)]
        pltpu.make_async_copy(piece, piece, sem).wait()

    def split(index):
        return index // (NX * NZ) * NX + lax.rem(index, NX), lax.rem(index // NX, NZ)

    def stage_plane(c):
        pltpu.make_async_copy(traces.at[0, part(0)], ra[c].at[0], own_sem.at[c]).wait()
        gathered(PLANE - 1, pa_recv.at[c])
        for h in range(NZ):
            sb[c, h] = ra[c][split(owner[h])[0]]
        for dz in range(1, NZ):
            device, _, z, _ = at(0, dz, 0)
            pltpu.make_async_remote_copy(
                src_ref=sb.at[c, z], dst_ref=rb[c].at[my_z],
                send_sem=pb_send.at[c], recv_sem=pb_recv.at[c], device_id={"shot": device}).start()
        rb[c][my_z] = sb[c, my_z]

    def unit(y, c):
        return (y * 4 + c) * NZ

    def stage_column(c):
        gathered(NZ - 1, pb_recv.at[c])
        mine = unit(my_y, c) + my_z
        win[mine] = rb[c][split(owner[my_z])[1]]
        for dz in range(1, NZ):
            device = at(0, dz, 0)[0]
            pltpu.make_async_remote_copy(
                src_ref=win.at[mine], dst_ref=win.at[mine],
                send_sem=zg_send.at[c], recv_sem=zg_recv.at[c], device_id={"shot": device}).start()

    def send_y(y, low, count, c, sem, away):
        piece = win.at[pl.ds(unit(y, c) + low, count)]
        pltpu.make_async_remote_copy(
            src_ref=piece, dst_ref=piece, send_sem=y_send.at[c], recv_sem=sem,
            device_id={"shot": at(away, 0, 0)[0]}).start()

    def arrive_y(y, low, count, c, sem):
        piece = win.at[pl.ds(unit(y, c) + low, count)]
        pltpu.make_async_copy(piece, piece, sem).wait()

    sides = ((0, 1), (1, 3))

    def stage_own(c):
        gathered(NZ - 1, zg_recv.at[c])
        for side, away in sides:
            send_y(my_y, 0, 4, c, y1.at[c, side], away)

    def stage_near(c):
        for side, away in sides:
            y = at(4 - away, 0, 0)[1]
            arrive_y(y, 0, 4, c, y1.at[c, side])
            send_y(y, 2 * side, 2, c, y2.at[c, side], away)

    def stage_far(c):
        y = at(2, 0, 0)[1]
        for side, _ in sides:
            arrive_y(y, 2 * side, 2, c, y2.at[c, side])

    def stack(c):
        for y in range(NY):
            tiles = [win[unit(y, c) + h] for h in range(4)]
            for b in range(4):
                lhs[b * size:(b + 1) * size, y * 4 * TAPS:(y + 1) * 4 * TAPS] = jnp.concatenate(
                    [t[:, b * TAPS:(b + 1) * TAPS] for t in tiles], axis=1)

    def product(x, c):
        return jnp.dot(lhs[...], band[x, c * deep:(c + 1) * deep, :], preferred_element_type=jnp.float32)

    def compute(c):
        stack(c)

        def body(x, carry):
            if c == 0:
                acc[x] = product(x, c)
            else:
                acc[x] += product(x, c)
            return carry

        lax.fori_loop(0, NX, body, 0)

    def finish(dx):
        device, _, _, x = at(0, 0, dx)
        acc[x] += product(x, CHUNKS - 1)
        lane = lax.broadcasted_iota(jnp.int32, (size, LANES), 1)
        for s in range(shots):
            a = [acc[x, b * size:(b + 1) * size, s * LANES:(s + 1) * LANES] for b in range(4)]
            odd, last = pltpu.roll(a[1], TAPS, 1), pltpu.roll(a[3], TAPS, 1)
            low = a[0] + jnp.where(lane >= TAPS, odd, 0.0)
            high = a[2] + jnp.where(lane < TAPS, odd, last)
            for half, value in ((0, low), (1, high)):
                span = slice(half * LANES, (half + 1) * LANES)
                res[x, s, :, span] = (held[x, s, :, span].astype(jnp.float32) - value).astype(jnp.bfloat16)
        if dx:
            pltpu.make_async_remote_copy(
                src_ref=res.at[x], dst_ref=out.at[:, part(my_x)], send_sem=o_send.at[dx], recv_sem=o_recv.at[dx],
                device_id={"shot": device}).start()
        else:
            pltpu.make_async_copy(res.at[x], out.at[:, part(my_x)], o_own).start()

    responses_x()
    stage_plane(0)
    responses_rcv()
    make_bands(0)
    stage_column(0)
    make_bands(1)
    stage_plane(1)
    stage_own(0)
    stage_column(1)
    make_bands(2)
    stage_plane(2)
    stage_near(0)
    stage_own(1)
    stage_column(2)
    stage_far(0)
    make_bands(3)
    stage_plane(3)
    stage_near(1)
    stage_own(2)
    stage_far(1)
    compute(0)
    stage_column(3)
    stage_near(2)
    compute(1)
    stage_own(3)
    stage_far(2)
    compute(2)
    stage_near(3)
    pltpu.make_async_copy(data.at[:, part(0)], held.at[0], d_own).wait()
    for dx in range(1, NX):
        pltpu.make_async_copy(data.at[:, part(0)], held.at[0], d_recv.at[dx]).wait()
    stage_far(3)
    stack(3)
    for dx in (2, 1, 3, 0):
        finish(dx)

    for dx in range(1, NX):
        pltpu.make_async_copy(prim_in, prim.at[0, 0], px_send.at[dx]).wait()
        pltpu.make_async_copy(data.at[:, part(0)], held.at[0], d_send.at[dx]).wait()
    for dr in range(1, NR):
        pltpu.make_async_copy(prim.at[0], prim.at[0], pr_send.at[dr]).wait()
    for c in range(CHUNKS):
        gathered(PLANE - 1, pa_send.at[c])
        gathered(NZ - 1, pb_send.at[c])
        gathered(NZ - 1, zg_send.at[c])
        gathered(12, y_send.at[c])
    pltpu.make_async_copy(res.at[0], out.at[:, part(0)], o_own).wait()
    for dx in range(1, NX):
        pltpu.make_async_copy(res.at[0], out.at[:, part(0)], o_send.at[dx]).wait()
        pltpu.make_async_copy(res.at[0], out.at[:, part(0)], o_recv.at[dx]).wait()


def shards(data, surface_traces, primaries, panel_owner):
    shots, rows, length = data.shape
    points = surface_traces.shape[0]
    size = rows // NX
    dma = pltpu.SemaphoreType.DMA
    anywhere = pl.BlockSpec(memory_space=pl.ANY)
    return pl.pallas_call(
        kernel,
        out_shape=jax.ShapeDtypeStruct(data.shape, jnp.bfloat16),
        in_specs=[pl.BlockSpec(memory_space=pltpu.SMEM), anywhere, pl.BlockSpec(memory_space=pltpu.VMEM), anywhere],
        out_specs=anywhere,
        scratch_shapes=[
            [pltpu.VMEM((PLANE, size, length), jnp.bfloat16)] * CHUNKS,
            pltpu.VMEM((CHUNKS, NZ, size, length), jnp.bfloat16),
            [pltpu.VMEM((NZ, size, length), jnp.bfloat16)] * CHUNKS,
            pltpu.VMEM((PLANE * NZ, size, length), jnp.bfloat16),
            pltpu.VMEM((NR, NX) + primaries.shape, jnp.bfloat16),
            pltpu.VMEM((NR, NX, shots, points, LANES), jnp.float32),
            pltpu.VMEM((NX, PLANE * 4 * TAPS, shots * LANES), jnp.bfloat16),
            pltpu.VMEM((4 * size, NY * 4 * TAPS), jnp.bfloat16),
            pltpu.VMEM((NX, 4 * size, shots * LANES), jnp.float32),
            pltpu.VMEM((NX, shots, size, length), jnp.bfloat16),
            pltpu.VMEM((NX, shots, size, length), jnp.bfloat16),
            dma((CHUNKS,)), dma((CHUNKS,)), dma((CHUNKS,)), dma((CHUNKS,)), dma((CHUNKS,)), dma((CHUNKS,)), dma((CHUNKS,)),
            dma, dma((NX,)), dma((NX,)), dma((NR,)), dma((NR,)),
            dma((CHUNKS,)), dma((CHUNKS, 2)), dma((CHUNKS, 2)),
            dma, dma((NX,)), dma((NX,)), dma, dma((NX,)), dma((NX,)),
        ],
        compiler_params=pltpu.CompilerParams(
            collective_id=0, has_side_effects=True, vmem_limit_bytes=60 * 1024 * 1024),
    )(panel_owner, surface_traces, primaries, data)


def solution(mesh):
    placed = (P("shot", "rcv", None), P("shot", "rcv", None), P("shot", "rcv", None), P())
    return jax.shard_map(
        shards, mesh=mesh, in_specs=placed, out_specs=P("shot", "rcv", None), check_vma=False
    )
```

```python
import jax
import jax.numpy as jnp
from jax import lax
from jax.experimental import pallas as pl
from jax.experimental.pallas import tpu as pltpu
from jax.sharding import PartitionSpec as P

NY, NZ, NX = 4, 4, 4
NR = 4
PLANE = NY * NX
TAPS = 64
LANES = 128
HALVES = 2
POINTS = 4
CHUNKS = HALVES * POINTS
COLUMN, OWN, NEAR, FAR = 2, 4, 6, 7


def kernel(owner, traces, prim_in, data, out, ra, sb, rb, win, prim, prim32, band, lhs, acc, held, res,
           own_sem, pa_send, pa_recv, pb_send, pb_recv, zg_send, zg_recv,
           px_own, px_send, px_recv, pr_send, pr_recv, y_send, y1, y2, d_own, d_send, d_recv, o_own, o_send, o_recv):
    shots, rows, length = data.shape
    size = rows // (NX * HALVES)
    deep = NY * 4 * TAPS
    shot = lax.axis_index("shot")
    rcv = lax.axis_index("rcv")
    my_x = lax.rem(shot, NX)
    my_z = lax.rem(shot // NX, NZ)
    my_y = shot // (NX * NZ)
    my_q = my_y * NX + my_x

    def at(dy, dz, dx):
        y = lax.rem(my_y + dy, NY)
        z = lax.rem(my_z + dz, NZ)
        x = lax.rem(my_x + dx, NX)
        return (y * NZ + z) * NX + x, y, z, x

    def part(x, half):
        return pl.ds(pl.multiple_of(x * (size * HALVES) + half * size, size), size)

    plane = [(dy, dx) for dy in range(NY) for dx in range(NX) if dy or dx]
    order = sorted(plane, key=lambda d: -(min(d[0], NY - d[0]) + min(d[1], NX - d[1])))

    barrier = pltpu.get_barrier_semaphore()
    for dy, dx in plane:
        pl.semaphore_signal(barrier, inc=1, device_id={"shot": at(dy, 0, dx)[0]})
    for dz in range(1, NZ):
        pl.semaphore_signal(barrier, inc=1, device_id={"shot": at(0, dz, 0)[0]})
    for dr in range(1, NR):
        pl.semaphore_signal(barrier, inc=1, device_id={"rcv": lax.rem(rcv + dr, NR)})
    pltpu.make_async_copy(prim_in, prim.at[rcv, my_x], px_own).start()
    for c in range(CHUNKS):
        half, k = divmod(c, POINTS)
        pltpu.make_async_copy(traces.at[my_y * POINTS + k, part(my_x, half)], ra[c].at[my_q], own_sem.at[c]).start()
    for half in range(HALVES):
        pltpu.make_async_copy(data.at[:, part(my_x, half)], held.at[half, my_x], d_own.at[half]).start()
    pl.semaphore_wait(barrier, len(plane) + NZ - 1 + NR - 1)

    for dx in range(1, NX):
        pltpu.make_async_remote_copy(
            src_ref=prim_in, dst_ref=prim.at[rcv, my_x], send_sem=px_send.at[dx], recv_sem=px_recv.at[dx],
            device_id={"shot": at(0, 0, dx)[0]}).start()

    for c in range(CHUNKS):
        half, k = divmod(c, POINTS)
        for dy, dx in order:
            device, y, _, x = at(dy, 0, dx)
            pltpu.make_async_remote_copy(
                src_ref=traces.at[y * POINTS + k, part(x, half)], dst_ref=ra[c].at[my_q],
                send_sem=pa_send.at[c], recv_sem=pa_recv.at[c], device_id={"shot": device}).start()

    for half in range(HALVES):
        for dx in (2, 1, 3):
            device, _, _, x = at(0, 0, dx)
            pltpu.make_async_remote_copy(
                src_ref=data.at[:, part(x, half)], dst_ref=held.at[half, my_x],
                send_sem=d_send.at[half, dx], recv_sem=d_recv.at[half, dx], device_id={"shot": device}).start()

    def responses_x():
        pltpu.make_async_copy(prim_in, prim.at[rcv, my_x], px_own).wait()
        for dx in range(1, NX):
            pltpu.make_async_copy(prim_in, prim.at[rcv, my_x], px_recv.at[dx]).wait()
        for dr in range(1, NR):
            pltpu.make_async_remote_copy(
                src_ref=prim.at[rcv], dst_ref=prim.at[rcv], send_sem=pr_send.at[dr], recv_sem=pr_recv.at[dr],
                device_id={"rcv": lax.rem(rcv + dr, NR)}).start()

    def responses_rcv():
        for dr in range(1, NR):
            pltpu.make_async_copy(prim.at[0], prim.at[0], pr_recv.at[dr]).wait()
        prim32[...] = jnp.zeros_like(prim32)
        prim32[:, :, :, :, 0:TAPS] = prim[...].astype(jnp.float32)

    def make_bands(k):
        def body(step, carry):
            x, y = step // NY, lax.rem(step, NY)
            for h in range(4):
                for s in range(shots):
                    row = prim32[h, x, s, pl.ds(y * POINTS + k, 1), :]
                    tile = pltpu.roll(jnp.broadcast_to(row, (TAPS, LANES)), 0, 1, stride=1, stride_axis=0)
                    start = pl.multiple_of(k * deep + y * (4 * TAPS) + h * TAPS, TAPS)
                    band[x, pl.ds(start, TAPS), s * LANES:(s + 1) * LANES] = tile.astype(jnp.bfloat16)
            return carry

        lax.fori_loop(0, NX * NY, body, 0)

    def gathered(count, sem):
        piece = win.at[pl.ds(0, count)]
        pltpu.make_async_copy(piece, piece, sem).wait()

    def split(index):
        return index // (NX * NZ) * NX + lax.rem(index, NX), lax.rem(index // NX, NZ)

    def stage_plane(c):
        pltpu.make_async_copy(traces.at[0, part(0, 0)], ra[c].at[0], own_sem.at[c]).wait()
        gathered(PLANE - 1, pa_recv.at[c])
        for h in range(NZ):
            sb[c, h] = ra[c][split(owner[h])[0]]
        for dz in range(1, NZ):
            device, _, z, _ = at(0, dz, 0)
            pltpu.make_async_remote_copy(
                src_ref=sb.at[c, z], dst_ref=rb[c].at[my_z],
                send_sem=pb_send.at[c], recv_sem=pb_recv.at[c], device_id={"shot": device}).start()
        rb[c][my_z] = sb[c, my_z]

    def unit(y, c):
        half, k = divmod(c, POINTS)
        return ((half * NY + y) * POINTS + k) * NZ

    def stage_column(c):
        gathered(NZ - 1, pb_recv.at[c])
        mine = unit(my_y, c) + my_z
        win[mine] = rb[c][split(owner[my_z])[1]]
        for dz in range(1, NZ):
            device = at(0, dz, 0)[0]
            pltpu.make_async_remote_copy(
                src_ref=win.at[mine], dst_ref=win.at[mine],
                send_sem=zg_send.at[c], recv_sem=zg_recv.at[c], device_id={"shot": device}).start()

    def send_y(y, low, count, c, sem, away):
        piece = win.at[pl.ds(unit(y, c) + low, count)]
        pltpu.make_async_remote_copy(
            src_ref=piece, dst_ref=piece, send_sem=y_send.at[c], recv_sem=sem,
            device_id={"shot": at(away, 0, 0)[0]}).start()

    def arrive_y(y, low, count, c, sem):
        piece = win.at[pl.ds(unit(y, c) + low, count)]
        pltpu.make_async_copy(piece, piece, sem).wait()

    sides = ((0, 1), (1, 3))

    def stage_own(c):
        gathered(NZ - 1, zg_recv.at[c])
        for side, away in sides:
            send_y(my_y, 0, 4, c, y1.at[c, side], away)

    def stage_near(c):
        for side, away in sides:
            y = at(4 - away, 0, 0)[1]
            arrive_y(y, 0, 4, c, y1.at[c, side])
            send_y(y, 2 * side, 2, c, y2.at[c, side], away)

    def stage_far(c):
        y = at(2, 0, 0)[1]
        for side, _ in sides:
            arrive_y(y, 2 * side, 2, c, y2.at[c, side])

    def stack(c):
        for y in range(NY):
            tiles = [win[unit(y, c) + h] for h in range(4)]
            for b in range(4):
                lhs[b * size:(b + 1) * size, y * 4 * TAPS:(y + 1) * 4 * TAPS] = jnp.concatenate(
                    [t[:, b * TAPS:(b + 1) * TAPS] for t in tiles], axis=1)

    def product(x, k):
        return jnp.dot(lhs[...], band[x, k * deep:(k + 1) * deep, :], preferred_element_type=jnp.float32)

    def compute(c):
        half, k = divmod(c, POINTS)
        stack(c)
        if k == POINTS - 1:
            for dx in range(NX):
                if dx == 0:
                    pltpu.make_async_copy(data.at[:, part(0, 0)], held.at[0, 0], d_own.at[half]).wait()
                else:
                    pltpu.make_async_copy(data.at[:, part(0, 0)], held.at[0, 0], d_recv.at[half, dx]).wait()
            for dx in (2, 1, 3, 0):
                finish(half, dx)
            return

        def body(x, carry):
            if k == 0:
                acc[x] = product(x, k)
            else:
                acc[x] += product(x, k)
            return carry

        lax.fori_loop(0, NX, body, 0)

    def finish(half, dx):
        device, _, _, x = at(0, 0, dx)
        acc[x] += product(x, POINTS - 1)
        lane = lax.broadcasted_iota(jnp.int32, (size, LANES), 1)
        for s in range(shots):
            a = [acc[x, b * size:(b + 1) * size, s * LANES:(s + 1) * LANES] for b in range(4)]
            odd, last = pltpu.roll(a[1], TAPS, 1), pltpu.roll(a[3], TAPS, 1)
            low = a[0] + jnp.where(lane >= TAPS, odd, 0.0)
            high = a[2] + jnp.where(lane < TAPS, odd, last)
            for side, value in ((0, low), (1, high)):
                span = slice(side * LANES, (side + 1) * LANES)
                res[half, x, s, :, span] = (held[half, x, s, :, span].astype(jnp.float32) - value).astype(jnp.bfloat16)
        if dx:
            pltpu.make_async_remote_copy(
                src_ref=res.at[half, x], dst_ref=out.at[:, part(my_x, half)],
                send_sem=o_send.at[half, dx], recv_sem=o_recv.at[half, dx], device_id={"shot": device}).start()
        else:
            pltpu.make_async_copy(res.at[half, x], out.at[:, part(my_x, half)], o_own.at[half]).start()

    responses_x()
    for slot in range(CHUNKS + FAR):
        for behind, stage in ((FAR, stage_far), (NEAR, stage_near), (OWN, stage_own), (COLUMN, stage_column), (0, stage_plane)):
            if 0 <= slot - behind < CHUNKS:
                stage(slot - behind)
        if slot == 0:
            responses_rcv()
        if 1 <= slot <= POINTS:
            make_bands(slot - 1)
        if slot >= FAR:
            compute(slot - FAR)

    for dx in range(1, NX):
        pltpu.make_async_copy(prim_in, prim.at[0, 0], px_send.at[dx]).wait()
        for half in range(HALVES):
            pltpu.make_async_copy(data.at[:, part(0, 0)], held.at[0, 0], d_send.at[half, dx]).wait()
    for dr in range(1, NR):
        pltpu.make_async_copy(prim.at[0], prim.at[0], pr_send.at[dr]).wait()
    for c in range(CHUNKS):
        gathered(PLANE - 1, pa_send.at[c])
        gathered(NZ - 1, pb_send.at[c])
        gathered(NZ - 1, zg_send.at[c])
        gathered(12, y_send.at[c])
    for half in range(HALVES):
        pltpu.make_async_copy(res.at[0, 0], out.at[:, part(0, 0)], o_own.at[half]).wait()
        for dx in range(1, NX):
            pltpu.make_async_copy(res.at[0, 0], out.at[:, part(0, 0)], o_send.at[half, dx]).wait()
            pltpu.make_async_copy(res.at[0, 0], out.at[:, part(0, 0)], o_recv.at[half, dx]).wait()


def shards(data, surface_traces, primaries, panel_owner):
    shots, rows, length = data.shape
    points = surface_traces.shape[0]
    size = rows // (NX * HALVES)
    dma = pltpu.SemaphoreType.DMA
    anywhere = pl.BlockSpec(memory_space=pl.ANY)
    return pl.pallas_call(
        kernel,
        out_shape=jax.ShapeDtypeStruct(data.shape, jnp.bfloat16),
        in_specs=[pl.BlockSpec(memory_space=pltpu.SMEM), anywhere, pl.BlockSpec(memory_space=pltpu.VMEM), anywhere],
        out_specs=anywhere,
        scratch_shapes=[
            [pltpu.VMEM((PLANE, size, length), jnp.bfloat16)] * CHUNKS,
            pltpu.VMEM((CHUNKS, NZ, size, length), jnp.bfloat16),
            [pltpu.VMEM((NZ, size, length), jnp.bfloat16)] * CHUNKS,
            pltpu.VMEM((HALVES * PLANE * NZ, size, length), jnp.bfloat16),
            pltpu.VMEM((NR, NX) + primaries.shape, jnp.bfloat16),
            pltpu.VMEM((NR, NX, shots, points, LANES), jnp.float32),
            pltpu.VMEM((NX, PLANE * 4 * TAPS, shots * LANES), jnp.bfloat16),
            pltpu.VMEM((4 * size, NY * 4 * TAPS), jnp.bfloat16),
            pltpu.VMEM((NX, 4 * size, shots * LANES), jnp.float32),
            pltpu.VMEM((HALVES, NX, shots, size, length), jnp.bfloat16),
            pltpu.VMEM((HALVES, NX, shots, size, length), jnp.bfloat16),
            dma((CHUNKS,)), dma((CHUNKS,)), dma((CHUNKS,)), dma((CHUNKS,)), dma((CHUNKS,)), dma((CHUNKS,)), dma((CHUNKS,)),
            dma, dma((NX,)), dma((NX,)), dma((NR,)), dma((NR,)),
            dma((CHUNKS,)), dma((CHUNKS, 2)), dma((CHUNKS, 2)),
            dma((HALVES,)), dma((HALVES, NX)), dma((HALVES, NX)), dma((HALVES,)), dma((HALVES, NX)), dma((HALVES, NX)),
        ],
        compiler_params=pltpu.CompilerParams(
            collective_id=0, has_side_effects=True, vmem_limit_bytes=60 * 1024 * 1024),
    )(panel_owner, surface_traces, primaries, data)


def solution(mesh):
    placed = (P("shot", "rcv", None), P("shot", "rcv", None), P("shot", "rcv", None), P())
    return jax.shard_map(
        shards, mesh=mesh, in_specs=placed, out_specs=P("shot", "rcv", None), check_vma=False
    )
```

```python
import jax
import jax.numpy as jnp
from jax import lax
from jax.experimental import pallas as pl
from jax.experimental.pallas import tpu as pltpu
from jax.sharding import PartitionSpec as P

NY, NZ, NX = 4, 4, 4
NR = 4
PLANE = NY * NX
TAPS = 64
LANES = 128
HALVES = 2
GROUP = 2
POINTS = 4 // GROUP
CHUNKS = HALVES * POINTS
COLUMN, OWN, NEAR, FAR = 2, 3, 4, 5


def kernel(owner, traces, prim_in, data, out, ra, sb, rb, win, prim, prim32, band, lhs, acc, held, res,
           own_sem, pa_send, pa_recv, pb_send, pb_recv, zg_send, zg_recv,
           px_own, px_send, px_recv, pr_send, pr_recv, y_send, y1, y2, d_own, d_send, d_recv, o_own, o_send, o_recv):
    shots, rows, length = data.shape
    size = rows // (NX * HALVES)
    deep = NY * 4 * TAPS
    shot = lax.axis_index("shot")
    rcv = lax.axis_index("rcv")
    my_x = lax.rem(shot, NX)
    my_z = lax.rem(shot // NX, NZ)
    my_y = shot // (NX * NZ)
    my_q = my_y * NX + my_x

    def at(dy, dz, dx):
        y = lax.rem(my_y + dy, NY)
        z = lax.rem(my_z + dz, NZ)
        x = lax.rem(my_x + dx, NX)
        return (y * NZ + z) * NX + x, y, z, x

    def part(x, half):
        return pl.ds(pl.multiple_of(x * (size * HALVES) + half * size, size), size)

    plane = [(dy, dx) for dy in range(NY) for dx in range(NX) if dy or dx]
    order = sorted(plane, key=lambda d: -(min(d[0], NY - d[0]) + min(d[1], NX - d[1])))

    barrier = pltpu.get_barrier_semaphore()
    for dy, dx in plane:
        pl.semaphore_signal(barrier, inc=1, device_id={"shot": at(dy, 0, dx)[0]})
    for dz in range(1, NZ):
        pl.semaphore_signal(barrier, inc=1, device_id={"shot": at(0, dz, 0)[0]})
    for dr in range(1, NR):
        pl.semaphore_signal(barrier, inc=1, device_id={"rcv": lax.rem(rcv + dr, NR)})
    pltpu.make_async_copy(prim_in, prim.at[rcv, my_x], px_own).start()
    for c in range(CHUNKS):
        half, k = divmod(c, POINTS)
        pltpu.make_async_copy(traces.at[pl.ds(my_y * 4 + k * GROUP, GROUP), part(my_x, half)], ra[c].at[my_q], own_sem.at[c]).start()
    for half in range(HALVES):
        pltpu.make_async_copy(data.at[:, part(my_x, half)], held.at[half, my_x], d_own.at[half]).start()
    pl.semaphore_wait(barrier, len(plane) + NZ - 1 + NR - 1)

    for dx in range(1, NX):
        pltpu.make_async_remote_copy(
            src_ref=prim_in, dst_ref=prim.at[rcv, my_x], send_sem=px_send.at[dx], recv_sem=px_recv.at[dx],
            device_id={"shot": at(0, 0, dx)[0]}).start()

    for c in range(CHUNKS):
        half, k = divmod(c, POINTS)
        for dy, dx in order:
            device, y, _, x = at(dy, 0, dx)
            pltpu.make_async_remote_copy(
                src_ref=traces.at[pl.ds(y * 4 + k * GROUP, GROUP), part(x, half)], dst_ref=ra[c].at[my_q],
                send_sem=pa_send.at[c], recv_sem=pa_recv.at[c], device_id={"shot": device}).start()

    for half in range(HALVES):
        for dx in (2, 1, 3):
            device, _, _, x = at(0, 0, dx)
            pltpu.make_async_remote_copy(
                src_ref=data.at[:, part(x, half)], dst_ref=held.at[half, my_x],
                send_sem=d_send.at[half, dx], recv_sem=d_recv.at[half, dx], device_id={"shot": device}).start()

    def responses_x():
        pltpu.make_async_copy(prim_in, prim.at[rcv, my_x], px_own).wait()
        for dx in range(1, NX):
            pltpu.make_async_copy(prim_in, prim.at[rcv, my_x], px_recv.at[dx]).wait()
        for dr in range(1, NR):
            pltpu.make_async_remote_copy(
                src_ref=prim.at[rcv], dst_ref=prim.at[rcv], send_sem=pr_send.at[dr], recv_sem=pr_recv.at[dr],
                device_id={"rcv": lax.rem(rcv + dr, NR)}).start()

    def responses_rcv():
        for dr in range(1, NR):
            pltpu.make_async_copy(prim.at[0], prim.at[0], pr_recv.at[dr]).wait()
        prim32[...] = jnp.zeros_like(prim32)
        prim32[:, :, :, :, 0:TAPS] = prim[...].astype(jnp.float32)

    def make_bands(k):
        def body(step, carry):
            x, y = step // NY, lax.rem(step, NY)
            for h in range(4):
                for s in range(shots):
                    row = prim32[h, x, s, pl.ds(y * 4 + k, 1), :]
                    tile = pltpu.roll(jnp.broadcast_to(row, (TAPS, LANES)), 0, 1, stride=1, stride_axis=0)
                    start = pl.multiple_of(k * deep + y * (4 * TAPS) + h * TAPS, TAPS)
                    band[x, pl.ds(start, TAPS), s * LANES:(s + 1) * LANES] = tile.astype(jnp.bfloat16)
            return carry

        lax.fori_loop(0, NX * NY, body, 0)

    def gathered(count, sem):
        piece = win.at[pl.ds(0, count)]
        pltpu.make_async_copy(piece, piece, sem).wait()

    def split(index):
        return index // (NX * NZ) * NX + lax.rem(index, NX), lax.rem(index // NX, NZ)

    def stage_plane(c):
        pltpu.make_async_copy(traces.at[pl.ds(0, GROUP), part(0, 0)], ra[c].at[0], own_sem.at[c]).wait()
        gathered(PLANE - 1, pa_recv.at[c])
        for h in range(NZ):
            sb[c, h] = ra[c][split(owner[h])[0]]
        for dz in range(1, NZ):
            device, _, z, _ = at(0, dz, 0)
            pltpu.make_async_remote_copy(
                src_ref=sb.at[c, z], dst_ref=rb[c].at[my_z],
                send_sem=pb_send.at[c], recv_sem=pb_recv.at[c], device_id={"shot": device}).start()
        rb[c][my_z] = sb[c, my_z]

    def unit(y, c):
        half, k = divmod(c, POINTS)
        return ((half * NY + y) * POINTS + k) * NZ

    def stage_column(c):
        gathered(NZ - 1, pb_recv.at[c])
        mine = unit(my_y, c) + my_z
        win[mine] = rb[c][split(owner[my_z])[1]]
        for dz in range(1, NZ):
            device = at(0, dz, 0)[0]
            pltpu.make_async_remote_copy(
                src_ref=win.at[mine], dst_ref=win.at[mine],
                send_sem=zg_send.at[c], recv_sem=zg_recv.at[c], device_id={"shot": device}).start()

    def send_y(y, low, count, c, sem, away):
        piece = win.at[pl.ds(unit(y, c) + low, count)]
        pltpu.make_async_remote_copy(
            src_ref=piece, dst_ref=piece, send_sem=y_send.at[c], recv_sem=sem,
            device_id={"shot": at(away, 0, 0)[0]}).start()

    def arrive_y(y, low, count, c, sem):
        piece = win.at[pl.ds(unit(y, c) + low, count)]
        pltpu.make_async_copy(piece, piece, sem).wait()

    sides = ((0, 1), (1, 3))

    def stage_own(c):
        gathered(NZ - 1, zg_recv.at[c])
        for side, away in sides:
            send_y(my_y, 0, 4, c, y1.at[c, side], away)

    def stage_near(c):
        for side, away in sides:
            y = at(4 - away, 0, 0)[1]
            arrive_y(y, 0, 4, c, y1.at[c, side])
            send_y(y, 2 * side, 2, c, y2.at[c, side], away)

    def stage_far(c):
        y = at(2, 0, 0)[1]
        for side, _ in sides:
            arrive_y(y, 2 * side, 2, c, y2.at[c, side])

    def stack(c):
        for y in range(NY):
            for i in range(GROUP):
                tiles = [win[unit(y, c) + h, i] for h in range(4)]
                start = i * deep + y * 4 * TAPS
                for b in range(4):
                    lhs[b * size:(b + 1) * size, start:start + 4 * TAPS] = jnp.concatenate(
                        [t[:, b * TAPS:(b + 1) * TAPS] for t in tiles], axis=1)

    def product(x, k):
        return jnp.dot(lhs[...], band[x, k * GROUP * deep:(k + 1) * GROUP * deep, :], preferred_element_type=jnp.float32)

    def compute(c):
        half, k = divmod(c, POINTS)
        stack(c)
        if k == POINTS - 1:
            for dx in range(NX):
                if dx == 0:
                    pltpu.make_async_copy(data.at[:, part(0, 0)], held.at[0, 0], d_own.at[half]).wait()
                else:
                    pltpu.make_async_copy(data.at[:, part(0, 0)], held.at[0, 0], d_recv.at[half, dx]).wait()
            for dx in (2, 1, 3, 0):
                finish(half, dx)
            return

        def body(x, carry):
            if k == 0:
                acc[x] = product(x, k)
            else:
                acc[x] += product(x, k)
            return carry

        lax.fori_loop(0, NX, body, 0)

    def finish(half, dx):
        device, _, _, x = at(0, 0, dx)
        acc[x] += product(x, POINTS - 1)
        lane = lax.broadcasted_iota(jnp.int32, (size, LANES), 1)
        for s in range(shots):
            a = [acc[x, b * size:(b + 1) * size, s * LANES:(s + 1) * LANES] for b in range(4)]
            odd, last = pltpu.roll(a[1], TAPS, 1), pltpu.roll(a[3], TAPS, 1)
            low = a[0] + jnp.where(lane >= TAPS, odd, 0.0)
            high = a[2] + jnp.where(lane < TAPS, odd, last)
            for side, value in ((0, low), (1, high)):
                span = slice(side * LANES, (side + 1) * LANES)
                res[half, x, s, :, span] = (held[half, x, s, :, span].astype(jnp.float32) - value).astype(jnp.bfloat16)
        if dx:
            pltpu.make_async_remote_copy(
                src_ref=res.at[half, x], dst_ref=out.at[:, part(my_x, half)],
                send_sem=o_send.at[half, dx], recv_sem=o_recv.at[half, dx], device_id={"shot": device}).start()
        else:
            pltpu.make_async_copy(res.at[half, x], out.at[:, part(my_x, half)], o_own.at[half]).start()

    responses_x()
    for slot in range(CHUNKS + FAR):
        for behind, stage in ((FAR, stage_far), (NEAR, stage_near), (OWN, stage_own), (COLUMN, stage_column), (0, stage_plane)):
            if 0 <= slot - behind < CHUNKS:
                stage(slot - behind)
        if slot == 0:
            responses_rcv()
        if 1 <= slot <= 4:
            make_bands(slot - 1)
        if slot >= FAR:
            compute(slot - FAR)

    for dx in range(1, NX):
        pltpu.make_async_copy(prim_in, prim.at[0, 0], px_send.at[dx]).wait()
        for half in range(HALVES):
            pltpu.make_async_copy(data.at[:, part(0, 0)], held.at[0, 0], d_send.at[half, dx]).wait()
    for dr in range(1, NR):
        pltpu.make_async_copy(prim.at[0], prim.at[0], pr_send.at[dr]).wait()
    for c in range(CHUNKS):
        gathered(PLANE - 1, pa_send.at[c])
        gathered(NZ - 1, pb_send.at[c])
        gathered(NZ - 1, zg_send.at[c])
        gathered(12, y_send.at[c])
    for half in range(HALVES):
        pltpu.make_async_copy(res.at[0, 0], out.at[:, part(0, 0)], o_own.at[half]).wait()
        for dx in range(1, NX):
            pltpu.make_async_copy(res.at[0, 0], out.at[:, part(0, 0)], o_send.at[half, dx]).wait()
            pltpu.make_async_copy(res.at[0, 0], out.at[:, part(0, 0)], o_recv.at[half, dx]).wait()


def shards(data, surface_traces, primaries, panel_owner):
    shots, rows, length = data.shape
    points = surface_traces.shape[0]
    size = rows // (NX * HALVES)
    dma = pltpu.SemaphoreType.DMA
    anywhere = pl.BlockSpec(memory_space=pl.ANY)
    return pl.pallas_call(
        kernel,
        out_shape=jax.ShapeDtypeStruct(data.shape, jnp.bfloat16),
        in_specs=[pl.BlockSpec(memory_space=pltpu.SMEM), anywhere, pl.BlockSpec(memory_space=pltpu.VMEM), anywhere],
        out_specs=anywhere,
        scratch_shapes=[
            [pltpu.VMEM((PLANE, GROUP, size, length), jnp.bfloat16)] * CHUNKS,
            pltpu.VMEM((CHUNKS, NZ, GROUP, size, length), jnp.bfloat16),
            [pltpu.VMEM((NZ, GROUP, size, length), jnp.bfloat16)] * CHUNKS,
            pltpu.VMEM((HALVES * NY * POINTS * NZ, GROUP, size, length), jnp.bfloat16),
            pltpu.VMEM((NR, NX) + primaries.shape, jnp.bfloat16),
            pltpu.VMEM((NR, NX, shots, points, LANES), jnp.float32),
            pltpu.VMEM((NX, PLANE * 4 * TAPS, shots * LANES), jnp.bfloat16),
            pltpu.VMEM((4 * size, GROUP * NY * 4 * TAPS), jnp.bfloat16),
            pltpu.VMEM((NX, 4 * size, shots * LANES), jnp.float32),
            pltpu.VMEM((HALVES, NX, shots, size, length), jnp.bfloat16),
            pltpu.VMEM((HALVES, NX, shots, size, length), jnp.bfloat16),
            dma((CHUNKS,)), dma((CHUNKS,)), dma((CHUNKS,)), dma((CHUNKS,)), dma((CHUNKS,)), dma((CHUNKS,)), dma((CHUNKS,)),
            dma, dma((NX,)), dma((NX,)), dma((NR,)), dma((NR,)),
            dma((CHUNKS,)), dma((CHUNKS, 2)), dma((CHUNKS, 2)),
            dma((HALVES,)), dma((HALVES, NX)), dma((HALVES, NX)), dma((HALVES,)), dma((HALVES, NX)), dma((HALVES, NX)),
        ],
        compiler_params=pltpu.CompilerParams(
            collective_id=0, has_side_effects=True, vmem_limit_bytes=60 * 1024 * 1024),
    )(panel_owner, surface_traces, primaries, data)


def solution(mesh):
    placed = (P("shot", "rcv", None), P("shot", "rcv", None), P("shot", "rcv", None), P())
    return jax.shard_map(
        shards, mesh=mesh, in_specs=placed, out_specs=P("shot", "rcv", None), check_vma=False
    )
```

```python
import jax
import jax.numpy as jnp
from jax import lax
from jax.experimental import pallas as pl
from jax.experimental.pallas import tpu as pltpu
from jax.sharding import PartitionSpec as P

NY, NZ, NX = 4, 4, 4
NR = 4
PLANE = NY * NX
TAPS = 64
LANES = 128
HALVES = 2
GROUP = 2
POINTS = 4 // GROUP
CHUNKS = HALVES * POINTS
COLUMN, OWN, NEAR, FAR = 2, 3, 4, 5


def kernel(owner, traces, prim_in, data, out, ra, sb, rb, win, prim, prim32, band, lhs, acc, held, res,
           own_sem, pa_send, pa_recv, pb_send, pb_recv, zg_send, zg_recv,
           px_own, px_send, px_recv, pr_send, pr_recv, y_send, y1, y2, d_own, d_send, d_recv, o_own, o_send, o_recv):
    shots, rows, length = data.shape
    size = rows // (NX * HALVES)
    deep = NY * 4 * TAPS
    shot = lax.axis_index("shot")
    rcv = lax.axis_index("rcv")
    my_x = lax.rem(shot, NX)
    my_z = lax.rem(shot // NX, NZ)
    my_y = shot // (NX * NZ)
    my_q = my_y * NX + my_x

    def at(dy, dz, dx):
        y = lax.rem(my_y + dy, NY)
        z = lax.rem(my_z + dz, NZ)
        x = lax.rem(my_x + dx, NX)
        return (y * NZ + z) * NX + x, y, z, x

    def part(x, half):
        return pl.ds(pl.multiple_of(x * (size * HALVES) + half * size, size), size)

    plane = [(dy, dx) for dy in range(NY) for dx in range(NX) if dy or dx]
    order = sorted(plane, key=lambda d: -(min(d[0], NY - d[0]) + min(d[1], NX - d[1])))

    barrier = pltpu.get_barrier_semaphore()
    for dy, dx in plane:
        pl.semaphore_signal(barrier, inc=1, device_id={"shot": at(dy, 0, dx)[0]})
    for dz in range(1, NZ):
        pl.semaphore_signal(barrier, inc=1, device_id={"shot": at(0, dz, 0)[0]})
    for dr in range(1, NR):
        pl.semaphore_signal(barrier, inc=1, device_id={"rcv": lax.rem(rcv + dr, NR)})
    pltpu.make_async_copy(prim_in, prim.at[rcv, my_x], px_own).start()
    for c in range(CHUNKS):
        half, k = divmod(c, POINTS)
        pltpu.make_async_copy(traces.at[pl.ds(my_y * 4 + k * GROUP, GROUP), part(my_x, half)], ra[c].at[my_q], own_sem.at[c]).start()
    for half in range(HALVES):
        pltpu.make_async_copy(data.at[:, part(my_x, half)], held.at[half, my_x], d_own.at[half]).start()
    pl.semaphore_wait(barrier, len(plane) + NZ - 1 + NR - 1)

    for dx in range(1, NX):
        pltpu.make_async_remote_copy(
            src_ref=prim_in, dst_ref=prim.at[rcv, my_x], send_sem=px_send.at[dx], recv_sem=px_recv.at[dx],
            device_id={"shot": at(0, 0, dx)[0]}).start()

    for c in range(CHUNKS):
        half, k = divmod(c, POINTS)
        for dy, dx in order:
            device, y, _, x = at(dy, 0, dx)
            pltpu.make_async_remote_copy(
                src_ref=traces.at[pl.ds(y * 4 + k * GROUP, GROUP), part(x, half)], dst_ref=ra[c].at[my_q],
                send_sem=pa_send.at[c], recv_sem=pa_recv.at[c], device_id={"shot": device}).start()

    for half in range(HALVES):
        for dx in (2, 1, 3):
            device, _, _, x = at(0, 0, dx)
            pltpu.make_async_remote_copy(
                src_ref=data.at[:, part(x, half)], dst_ref=held.at[half, my_x],
                send_sem=d_send.at[half, dx], recv_sem=d_recv.at[half, dx], device_id={"shot": device}).start()

    def responses_x():
        pltpu.make_async_copy(prim_in, prim.at[rcv, my_x], px_own).wait()
        for dx in range(1, NX):
            pltpu.make_async_copy(prim_in, prim.at[rcv, my_x], px_recv.at[dx]).wait()
        for dr in range(1, NR):
            pltpu.make_async_remote_copy(
                src_ref=prim.at[rcv], dst_ref=prim.at[rcv], send_sem=pr_send.at[dr], recv_sem=pr_recv.at[dr],
                device_id={"rcv": lax.rem(rcv + dr, NR)}).start()

    def responses_rcv():
        for dr in range(1, NR):
            pltpu.make_async_copy(prim.at[0], prim.at[0], pr_recv.at[dr]).wait()
        prim32[...] = jnp.zeros_like(prim32)
        prim32[:, :, :, :, 0:TAPS] = prim[...].astype(jnp.float32)

    def make_bands(k):
        def body(step, carry):
            x, y = step // NY, lax.rem(step, NY)
            for h in range(4):
                for s in range(shots):
                    row = prim32[h, x, s, pl.ds(y * 4 + k, 1), :]
                    tile = pltpu.roll(jnp.broadcast_to(row, (TAPS, LANES)), 0, 1, stride=1, stride_axis=0)
                    start = pl.multiple_of(k * deep + y * (4 * TAPS) + h * TAPS, TAPS)
                    band[x, pl.ds(start, TAPS), s * LANES:(s + 1) * LANES] = tile.astype(jnp.bfloat16)
            return carry

        lax.fori_loop(0, NX * NY, body, 0)

    def gathered(count, sem):
        piece = win.at[pl.ds(0, count)]
        pltpu.make_async_copy(piece, piece, sem).wait()

    def split(index):
        return index // (NX * NZ) * NX + lax.rem(index, NX), lax.rem(index // NX, NZ)

    def stage_plane(c):
        pltpu.make_async_copy(traces.at[pl.ds(0, GROUP), part(0, 0)], ra[c].at[0], own_sem.at[c]).wait()
        gathered(PLANE - 1, pa_recv.at[c])
        for h in range(NZ):
            sb[c, h] = ra[c][split(owner[h])[0]]
        for dz in (2, 1, 3):
            device, _, z, _ = at(0, dz, 0)
            pltpu.make_async_remote_copy(
                src_ref=sb.at[c, z], dst_ref=rb[c].at[my_z],
                send_sem=pb_send.at[c], recv_sem=pb_recv.at[c], device_id={"shot": device}).start()
        rb[c][my_z] = sb[c, my_z]

    def unit(y, c):
        half, k = divmod(c, POINTS)
        return ((half * NY + y) * POINTS + k) * NZ

    def stage_column(c):
        gathered(NZ - 1, pb_recv.at[c])
        mine = unit(my_y, c) + my_z
        win[mine] = rb[c][split(owner[my_z])[1]]
        for dz in (2, 1, 3):
            device = at(0, dz, 0)[0]
            pltpu.make_async_remote_copy(
                src_ref=win.at[mine], dst_ref=win.at[mine],
                send_sem=zg_send.at[c], recv_sem=zg_recv.at[c], device_id={"shot": device}).start()

    def send_y(y, low, count, c, sem, away):
        piece = win.at[pl.ds(unit(y, c) + low, count)]
        pltpu.make_async_remote_copy(
            src_ref=piece, dst_ref=piece, send_sem=y_send.at[c], recv_sem=sem,
            device_id={"shot": at(away, 0, 0)[0]}).start()

    def arrive_y(y, low, count, c, sem):
        piece = win.at[pl.ds(unit(y, c) + low, count)]
        pltpu.make_async_copy(piece, piece, sem).wait()

    sides = ((0, 1), (1, 3))

    def stage_own(c):
        gathered(NZ - 1, zg_recv.at[c])
        for side, away in sides:
            send_y(my_y, 0, 4, c, y1.at[c, side], away)

    def stage_near(c):
        for side, away in sides:
            y = at(4 - away, 0, 0)[1]
            arrive_y(y, 0, 4, c, y1.at[c, side])
            send_y(y, 2 * side, 2, c, y2.at[c, side], away)

    def stage_far(c):
        y = at(2, 0, 0)[1]
        for side, _ in sides:
            arrive_y(y, 2 * side, 2, c, y2.at[c, side])

    def stack(c):
        for y in range(NY):
            for i in range(GROUP):
                tiles = [win[unit(y, c) + h, i] for h in range(4)]
                start = i * deep + y * 4 * TAPS
                for b in range(4):
                    lhs[b * size:(b + 1) * size, start:start + 4 * TAPS] = jnp.concatenate(
                        [t[:, b * TAPS:(b + 1) * TAPS] for t in tiles], axis=1)

    def product(x, k):
        return jnp.dot(lhs[...], band[x, k * GROUP * deep:(k + 1) * GROUP * deep, :], preferred_element_type=jnp.float32)

    def compute(c):
        half, k = divmod(c, POINTS)
        stack(c)
        if k == POINTS - 1:
            for dx in range(NX):
                if dx == 0:
                    pltpu.make_async_copy(data.at[:, part(0, 0)], held.at[0, 0], d_own.at[half]).wait()
                else:
                    pltpu.make_async_copy(data.at[:, part(0, 0)], held.at[0, 0], d_recv.at[half, dx]).wait()
            for dx in (2, 1, 3, 0):
                finish(half, dx)
            return

        def body(x, carry):
            if k == 0:
                acc[x] = product(x, k)
            else:
                acc[x] += product(x, k)
            return carry

        lax.fori_loop(0, NX, body, 0)

    def finish(half, dx):
        device, _, _, x = at(0, 0, dx)
        acc[x] += product(x, POINTS - 1)
        lane = lax.broadcasted_iota(jnp.int32, (size, LANES), 1)
        for s in range(shots):
            a = [acc[x, b * size:(b + 1) * size, s * LANES:(s + 1) * LANES] for b in range(4)]
            odd, last = pltpu.roll(a[1], TAPS, 1), pltpu.roll(a[3], TAPS, 1)
            low = a[0] + jnp.where(lane >= TAPS, odd, 0.0)
            high = a[2] + jnp.where(lane < TAPS, odd, last)
            for side, value in ((0, low), (1, high)):
                span = slice(side * LANES, (side + 1) * LANES)
                res[half, x, s, :, span] = (held[half, x, s, :, span].astype(jnp.float32) - value).astype(jnp.bfloat16)
        if dx:
            pltpu.make_async_remote_copy(
                src_ref=res.at[half, x], dst_ref=out.at[:, part(my_x, half)],
                send_sem=o_send.at[half, dx], recv_sem=o_recv.at[half, dx], device_id={"shot": device}).start()
        else:
            pltpu.make_async_copy(res.at[half, x], out.at[:, part(my_x, half)], o_own.at[half]).start()

    responses_x()
    for slot in range(CHUNKS + FAR):
        for behind, stage in ((FAR, stage_far), (NEAR, stage_near), (OWN, stage_own), (COLUMN, stage_column), (0, stage_plane)):
            if 0 <= slot - behind < CHUNKS:
                stage(slot - behind)
        if slot == 0:
            responses_rcv()
        if 1 <= slot <= 4:
            make_bands(slot - 1)
        if slot >= FAR:
            compute(slot - FAR)

    for dx in range(1, NX):
        pltpu.make_async_copy(prim_in, prim.at[0, 0], px_send.at[dx]).wait()
        for half in range(HALVES):
            pltpu.make_async_copy(data.at[:, part(0, 0)], held.at[0, 0], d_send.at[half, dx]).wait()
    for dr in range(1, NR):
        pltpu.make_async_copy(prim.at[0], prim.at[0], pr_send.at[dr]).wait()
    for c in range(CHUNKS):
        gathered(PLANE - 1, pa_send.at[c])
        gathered(NZ - 1, pb_send.at[c])
        gathered(NZ - 1, zg_send.at[c])
        gathered(12, y_send.at[c])
    for half in range(HALVES):
        pltpu.make_async_copy(res.at[0, 0], out.at[:, part(0, 0)], o_own.at[half]).wait()
        for dx in range(1, NX):
            pltpu.make_async_copy(res.at[0, 0], out.at[:, part(0, 0)], o_send.at[half, dx]).wait()
            pltpu.make_async_copy(res.at[0, 0], out.at[:, part(0, 0)], o_recv.at[half, dx]).wait()


def shards(data, surface_traces, primaries, panel_owner):
    shots, rows, length = data.shape
    points = surface_traces.shape[0]
    size = rows // (NX * HALVES)
    dma = pltpu.SemaphoreType.DMA
    anywhere = pl.BlockSpec(memory_space=pl.ANY)
    return pl.pallas_call(
        kernel,
        out_shape=jax.ShapeDtypeStruct(data.shape, jnp.bfloat16),
        in_specs=[pl.BlockSpec(memory_space=pltpu.SMEM), anywhere, pl.BlockSpec(memory_space=pltpu.VMEM), anywhere],
        out_specs=anywhere,
        scratch_shapes=[
            [pltpu.VMEM((PLANE, GROUP, size, length), jnp.bfloat16)] * CHUNKS,
            pltpu.VMEM((CHUNKS, NZ, GROUP, size, length), jnp.bfloat16),
            [pltpu.VMEM((NZ, GROUP, size, length), jnp.bfloat16)] * CHUNKS,
            pltpu.VMEM((HALVES * NY * POINTS * NZ, GROUP, size, length), jnp.bfloat16),
            pltpu.VMEM((NR, NX) + primaries.shape, jnp.bfloat16),
            pltpu.VMEM((NR, NX, shots, points, LANES), jnp.float32),
            pltpu.VMEM((NX, PLANE * 4 * TAPS, shots * LANES), jnp.bfloat16),
            pltpu.VMEM((4 * size, GROUP * NY * 4 * TAPS), jnp.bfloat16),
            pltpu.VMEM((NX, 4 * size, shots * LANES), jnp.float32),
            pltpu.VMEM((HALVES, NX, shots, size, length), jnp.bfloat16),
            pltpu.VMEM((HALVES, NX, shots, size, length), jnp.bfloat16),
            dma((CHUNKS,)), dma((CHUNKS,)), dma((CHUNKS,)), dma((CHUNKS,)), dma((CHUNKS,)), dma((CHUNKS,)), dma((CHUNKS,)),
            dma, dma((NX,)), dma((NX,)), dma((NR,)), dma((NR,)),
            dma((CHUNKS,)), dma((CHUNKS, 2)), dma((CHUNKS, 2)),
            dma((HALVES,)), dma((HALVES, NX)), dma((HALVES, NX)), dma((HALVES,)), dma((HALVES, NX)), dma((HALVES, NX)),
        ],
        compiler_params=pltpu.CompilerParams(
            collective_id=0, has_side_effects=True, vmem_limit_bytes=60 * 1024 * 1024),
    )(panel_owner, surface_traces, primaries, data)


def solution(mesh):
    placed = (P("shot", "rcv", None), P("shot", "rcv", None), P("shot", "rcv", None), P())
    return jax.shard_map(
        shards, mesh=mesh, in_specs=placed, out_specs=P("shot", "rcv", None), check_vma=False
    )
```
